32 devices in a mesh: rep: 16 (over z, y, core), fsdp: 2 (over x).
Axes of the slice: x: 2, y: 2, z: 4, core: 2. Of those that a mesh axis runs over, the one named last changes fastest.
Arguments:
- tokens: bfloat16 [2, 16, 1024, 768], P(None, 'rep', 'fsdp'), may hold values from -6 to 6
- cotangent: bfloat16 [2, 16, 1024, 768], P(None, 'rep', 'fsdp'), may hold values from -6 to 6
- doc_ids: int32 [2, 16, 1024], P(None, 'rep'), may hold values from 0 to 3, never falling along the last dimension, each value on 1 to 512 neighbouring positions
- positions: int32 [2, 16, 128], P(None, 'rep'), may hold values from 0 to 1023, as said below
- w_qkv: bfloat16 [768, 2304], P('fsdp'), may hold values from -0.21875 to 0.21875
- w_out: bfloat16 [768, 768], P('fsdp'), may hold values from -0.625 to 0.625
- w_fc: bfloat16 [768, 3072], P('fsdp'), may hold values from -0.21875 to 0.21875
- w_proj: bfloat16 [3072, 768], P('fsdp'), may hold values from -0.109375 to 0.109375
- ln1_gain: bfloat16 [768], P('fsdp'), may hold values from 0.5 to 1.5
- ln1_bias: bfloat16 [768], P('fsdp'), may hold values from -0.796875 to 0.796875
- ln2_gain: bfloat16 [768], P('fsdp'), may hold values from 0.5 to 1.5
- ln2_bias: bfloat16 [768], P('fsdp'), may hold values from -0.796875 to 0.796875
- fc_bias: bfloat16 [3072], P('fsdp'), may hold values from -0.796875 to 0.796875
- proj_bias: bfloat16 [768], P('fsdp'), may hold values from -0.796875 to 0.796875
- mean_weight: bfloat16 [256, 12], P('fsdp'), may hold values from -0.375 to 0.375
- spread_weight: bfloat16 [256, 12], P('fsdp'), may hold values from -0.375 to 0.375
Outputs:
- output: bfloat16 [2, 16, 1024, 768], P(None, 'rep', 'fsdp')
- grad_tokens: float32 [2, 16, 1024, 768], P(None, 'rep', 'fsdp')
- grad_w_qkv: float32 [768, 2304], P('fsdp')
- grad_w_out: float32 [768, 768], P('fsdp')
- grad_w_fc: float32 [768, 3072], P('fsdp')
- grad_w_proj: float32 [3072, 768], P('fsdp')
- grad_ln1_gain: float32 [768], P('fsdp')
- grad_ln1_bias: float32 [768], P('fsdp')
- grad_ln2_gain: float32 [768], P('fsdp')
- grad_ln2_bias: float32 [768], P('fsdp')
- grad_fc_bias: float32 [3072], P('fsdp')
- grad_proj_bias: float32 [768], P('fsdp')
- grad_mean_weight: float32 [256, 12], P('fsdp')
- grad_spread_weight: float32 [256, 12], P('fsdp')
The draws below stay inside these ranges and needn't reach their ends.
Inputs may be any that keep to these rules, and one draw needn't show every extreme that they name: `positions`: samples 64 * j to 64 * (j + 1) - 1 of a sequence are distinct tokens of its j-th run of 512 tokens, among them the run's first and last token. `doc_ids`: A sequence's document numbers never fall along it; a document has at most 512 tokens.
All inputs are finite; a program needn't handle non-finite values.
Results may differ from the reference program's by a relative error of at most 0.019.
Values may be sent and summed in bfloat16 or wider, within the bound.
No kernel may reach another device: no remote copies, remote signals or barrier semaphores. Data moves between devices by JAX's collectives and lax.ppermute only.
A program may use at most 320 MiB of HBM per device.

```python
import math
import jax
import jax.numpy as jnp
import numpy as np
from jax import lax

D = 768
H = 12
HD = 64
FF = 3072
NB = 256
BLK = 256
MICRO = 2
TOK = 512
SD = 64
SEQ = 1024
SEQS = 16
SAMPLES = 128


def draw_positions(key, part):
    run_count = SAMPLES // SD
    total_runs = MICRO * SEQS * run_count

    def one_run(run_index):
        run_key = jax.random.fold_in(key, run_index)
        middle = jax.random.permutation(run_key, TOK - 2)[:SD - 2].astype(jnp.int32) + 1
        within = jnp.concatenate([jnp.array([0, TOK - 1], dtype=jnp.int32), middle])
        return within + run_index % run_count * TOK
    chosen = jax.vmap(one_run)(jnp.arange(total_runs, dtype=jnp.int32))
    return chosen.reshape(MICRO, SEQS, SAMPLES).astype(jnp.int32)


def spiked(values, rng, source, target, parts, factor):
    owner, partner = [(jnp.arange(values.shape[position]) // (values.shape[position] // parts)).reshape([-1 if axis == position else 1 for axis in range(values.ndim)]) for position in (source, target)]
    chosen = jax.random.permutation(rng, parts)[partner]
    strong = (owner == chosen) | (owner == (partner + parts // 2) % parts)
    return jnp.where(strong, factor * values, values)


def block_scale(key, shape, pieces, low, top_value):
    gain, own = 1.0, jax.random.fold_in(key, 6)
    for axis_at, blocks in pieces:
        steps = jnp.exp(jax.random.uniform(jax.random.fold_in(own, axis_at), (blocks,), jnp.float32, low / len(pieces), top_value / len(pieces)))
        gain = gain * jnp.repeat(steps, shape[axis_at] // blocks).reshape([-1 if axis == axis_at else 1 for axis in range(len(shape))])
    return gain


def profile(count, total, most, lean):
    weights = [(1 << 20) // math.isqrt(grade ** lean) + 1 for grade in range(2, count + 1)]
    spare, given = total - most - (count - 1), [1] * (count - 1)
    while spare > 0:
        movable = [i for i in range(count - 1) if given[i] < most]
        mass, budget = sum([weights[i] for i in movable]), spare
        for i in movable:
            extra = min(most - given[i], max(1, budget * weights[i] // mass), spare)
            given[i] = given[i] + extra
            spare = spare - extra
    return np.array([most] + given)


def ragged_sizes(rng, number_of, total, bound, lean):
    if number_of == 2:
        one = jax.random.randint(rng, (), max(1, total - bound), min(bound, total - 1) + 1)
        return jnp.stack([one, total - one])
    lengths = jnp.asarray(profile(number_of, total, bound, lean), jnp.int32)
    twos = (number_of - 1) // 2
    giver, taker = lengths[1:1 + 2 * twos:2], lengths[2:2 + 2 * twos:2]
    margin = jnp.minimum(giver - 1, bound - taker)
    shifted = jax.random.randint(jax.random.fold_in(rng, 1), (twos,), 0, 1 << 20) % (margin + 1)
    lengths = lengths.at[1:1 + 2 * twos:2].set(giver - shifted).at[2:2 + 2 * twos:2].set(taker + shifted)
    return lengths[jax.random.permutation(jax.random.fold_in(rng, 2), number_of)]


def noise(stream_key, extent, scale, bound, cuts=(), kind=jnp.bfloat16):
    values = jax.random.normal(stream_key, extent, jnp.float32) * scale
    if len(cuts) > 0:
        values = block_scale(stream_key, extent, cuts, -0.22, 0.18) * values
    return jnp.clip(values, min=-bound, max=bound).astype(kind)


def noise_with(own_key, dims, scale, limit, pieces, heavy, held_as=jnp.bfloat16):
    entries = scale * jax.random.normal(own_key, dims, jnp.float32)
    if pieces:
        entries = entries * block_scale(own_key, dims, pieces, -0.22, 0.18)
    return jnp.clip(spiked(entries, jax.random.fold_in(own_key, 3), *heavy), -limit, limit).astype(held_as)


def setup_inputs(seed: int = 0) -> dict:
    seeds = jax.random.split(jax.random.key(seed), 17)
    return {
        "tokens": noise_with(seeds[0], (MICRO, SEQS, SEQ, D), 1.0, 6.0, ((1, 16), (2, 2)), (1, 3, 16, 2.0)),
        "cotangent": noise(seeds[1], (MICRO, SEQS, SEQ, D), 1.0, 6.0, ((1, 16), (2, 2))),
        "doc_ids": jax.vmap(lambda own: jnp.searchsorted(jnp.cumsum(ragged_sizes(own, 4, SEQ, SEQ // 2, 0)), jnp.arange(SEQ), side="right"))(jax.random.split(seeds[2], MICRO * SEQS)).reshape((MICRO, SEQS, SEQ)).astype(jnp.int32),
        "positions": draw_positions(jax.random.fold_in(seeds[16], 71), 0),
        "w_qkv": noise(seeds[4], (D, 3 * D), D ** -0.5, 0.21875, ((0, 2),)),
        "w_out": noise(seeds[5], (D, D), (D // 8) ** -0.5, 0.625, ((0, 2),)),
        "w_fc": noise(seeds[6], (D, FF), D ** -0.5, 0.21875, ((0, 2),)),
        "w_proj": noise(seeds[7], (FF, D), FF ** -0.5, 0.109375, ((0, 2),)),
        "ln1_gain": jnp.clip(1.0 + 0.1 * jax.random.normal(seeds[8], (D,), jnp.float32), 0.5, 1.5).astype(jnp.bfloat16),
        "ln1_bias": noise(seeds[9], (D,), 0.2, 0.796875, ((0, 2),)),
        "ln2_gain": jnp.clip(1.0 + 0.1 * jax.random.normal(seeds[10], (D,), jnp.float32), 0.5, 1.5).astype(jnp.bfloat16),
        "ln2_bias": noise(seeds[11], (D,), 0.2, 0.796875, ((0, 2),)),
        "fc_bias": noise(seeds[12], (FF,), 0.2, 0.796875, ((0, 2),)),
        "proj_bias": noise(seeds[13], (D,), 0.2, 0.796875, ((0, 2),)),
        "mean_weight": noise(seeds[14], (NB, H), NB ** -0.5, 0.375, ((0, 2),)),
        "spread_weight": noise(seeds[15], (NB, H), NB ** -0.5, 0.375, ((0, 2),)),
    }


HIGHEST = lax.Precision.HIGHEST
EPSILON = 1e-05
RIDGE_TERM = 0.5
SIGMA_SCALE = 0.01
MASKED = -1e+30

@jax.custom_vjp
def low(v):
    return lax.optimization_barrier(v.astype(jnp.bfloat16)).astype(jnp.float32)

@jax.custom_vjp
def low_back(v):
    return v

def low_keep(v):
    return (low(v), None)

def low_pass(kept, grad):
    return (grad,)

def back_keep(v):
    return (v, None)

def back_low(kept, grad):
    return (low(grad),)
low.defvjp(low_keep, low_pass)
low_back.defvjp(back_keep, back_low)

def matmul(first_op, second_op):
    return jnp.dot(first_op.astype(jnp.float32), second_op.astype(jnp.float32), precision=HIGHEST, preferred_element_type=jnp.float32)

def layer_norm(inputs, gains, offsets):
    centred = inputs - lax.optimization_barrier(jnp.mean(inputs, axis=-1, keepdims=True))
    inv_std = lax.rsqrt(lax.optimization_barrier(jnp.mean(centred * centred, axis=-1, keepdims=True)) + EPSILON)
    return centred * inv_std * gains + offsets

def basis_rows(sample_pos, length, basis_count):
    times = (sample_pos.astype(jnp.float32) + 0.5) / length
    centres = (jnp.arange(basis_count, dtype=jnp.float32) + 0.5) / basis_count
    basis_width = 1.25 / basis_count
    return jnp.exp(-(times[:, None] - centres[None, :]) ** 2 / (2.0 * basis_width * basis_width))

def density_weights(scaled, mean_proj, spread_proj, basis_count):
    centres = (jnp.arange(basis_count, dtype=jnp.float32) + 0.5) / basis_count
    basis_var = (1.25 / basis_count) ** 2
    mean_logit = jnp.einsum('thn,nh->th', scaled, mean_proj, precision=HIGHEST)
    spread_logit = jnp.einsum('thn,nh->th', scaled, spread_proj, precision=HIGHEST)
    middle = jax.nn.sigmoid(mean_logit)
    spread_sq = basis_var + SIGMA_SCALE * jax.nn.softplus(spread_logit)
    amplitude = jnp.sqrt(basis_var / spread_sq)
    offset_sq = (middle[..., None] - centres) ** 2
    return amplitude[..., None] * jnp.exp(-offset_sq / (2.0 * spread_sq[..., None]))

def block_pattern(block):
    query_blk = jnp.arange(2 * block) // block + 1
    key_blk = jnp.arange(3 * block) // block
    return (key_blk[None, :] == query_blk[:, None]) | (key_blk[None, :] == query_blk[:, None] - 1)

def forward(inputs, weights, seq_docs, sample_pos):
    full_qkv, full_out, full_fc, full_proj, gain_first, bias_first, gain_second, bias_second, hidden_bias, output_bias, mean_proj, spread_proj = weights
    score_scale = HD ** (-0.5)
    first_low = low(layer_norm(inputs, gain_first, bias_first))
    qkv_all = low(low_back(matmul(first_low, full_qkv)))
    queries = qkv_all[:, :D].reshape(SEQ, H, HD)
    keyval = qkv_all[:, D:]
    basis_tab = basis_rows(sample_pos, SEQ, NB)
    system = matmul(basis_tab.T, basis_tab) + RIDGE_TERM * jnp.eye(NB, dtype=jnp.float32)
    factor = jnp.linalg.cholesky(system)
    picked = jnp.take(first_low, sample_pos, axis=0)
    coeffs = jax.scipy.linalg.cho_solve((factor, True), matmul(basis_tab.T, picked))
    coeff_low = low(low_back(coeffs))
    memory_kv = low(low_back(matmul(coeff_low, full_qkv[:, D:])))
    mem_keys = memory_kv[:, :D].reshape(NB, H, HD)
    mem_vals = memory_kv[:, D:].reshape(NB, H, HD)
    scaled = low_back(jnp.einsum('thd,nhd->thn', queries, mem_keys, precision=HIGHEST) * score_scale)
    density = low(density_weights(scaled, mean_proj, spread_proj, NB))
    mem_out = jnp.einsum('thn,nhd->thd', density, mem_vals, precision=HIGHEST).reshape(SEQ, D)
    ext_kv = jnp.concatenate([jnp.zeros((BLK, 2 * D), jnp.float32), keyval], axis=0)
    ext_docs = jnp.concatenate([jnp.full((BLK,), -1, jnp.int32), seq_docs.astype(jnp.int32)])
    pattern = block_pattern(BLK)

    @jax.checkpoint
    def attend_group(group_idx):
        row_start = (group_idx * 2 * BLK).astype(jnp.int32)
        q_part = lax.dynamic_slice_in_dim(queries, row_start, 2 * BLK)
        kv_part = lax.dynamic_slice_in_dim(ext_kv, row_start, 3 * BLK)
        key_docs = lax.dynamic_slice_in_dim(ext_docs, row_start, 3 * BLK)
        query_docs = lax.dynamic_slice_in_dim(seq_docs.astype(jnp.int32), row_start, 2 * BLK)
        allowed = pattern & (query_docs[:, None] == key_docs[None, :])
        key_part = kv_part[:, :D].reshape(3 * BLK, H, HD)
        val_part = kv_part[:, D:].reshape(3 * BLK, H, HD)
        raw_scores = low_back(jnp.einsum('qhd,khd->hqk', q_part, key_part, precision=HIGHEST) * score_scale)
        masked = jnp.where(allowed[None], raw_scores, MASKED)
        attn_prob = jax.nn.softmax(masked, axis=-1)
        return jnp.einsum('hqk,khd->qhd', low(attn_prob), val_part, precision=HIGHEST).reshape(2 * BLK, D)
    attended = lax.map(attend_group, jnp.arange(SEQ // (2 * BLK), dtype=jnp.int32)).reshape(SEQ, D)
    context = low(low_back(attended + mem_out))
    branch_out = low_back(matmul(context, full_out))
    residual = inputs + branch_out
    second_low = low(layer_norm(residual, gain_second, bias_second))
    pre_act = low_back(matmul(second_low, full_fc) + hidden_bias)
    act_low = low(jax.nn.gelu(pre_act, approximate=True))
    mlp_out = low_back(matmul(act_low, full_proj) + output_bias)
    return residual + mlp_out

def reference(tokens, cotangent, doc_ids, positions, w_qkv, w_out, w_fc, w_proj, ln1_gain, ln1_bias, ln2_gain, ln2_bias, fc_bias, proj_bias, mean_weight, spread_weight):
    params = tuple((param.astype(jnp.float32) for param in (w_qkv, w_out, w_fc, w_proj, ln1_gain, ln1_bias, ln2_gain, ln2_bias, fc_bias, proj_bias, mean_weight, spread_weight)))
    seq_count = MICRO * SEQS
    flat_tokens = tokens.reshape(seq_count, SEQ, D).astype(jnp.float32)
    flat_cot = cotangent.reshape(seq_count, SEQ, D).astype(jnp.float32)
    flat_docs = doc_ids.reshape(seq_count, SEQ).astype(jnp.int32)
    flat_pos = positions.reshape(seq_count, SAMPLES).astype(jnp.int32)

    def one_sequence(running, seq_items):
        seq_tokens, seq_cot, seq_docs, seq_pos = seq_items
        result, pullback = jax.vjp(lambda inputs, weights: forward(inputs, weights, seq_docs, seq_pos), seq_tokens, params)
        grad_inputs, grad_weights = pullback(seq_cot)
        running = jax.tree.map(jnp.add, running, grad_weights)
        return (running, (result.astype(jnp.bfloat16), grad_inputs))
    zeros_init = jax.tree.map(jnp.zeros_like, params)
    totals, (outputs, grads_in) = lax.scan(one_sequence, zeros_init, (flat_tokens, flat_cot, flat_docs, flat_pos))
    return (outputs.reshape(MICRO, SEQS, SEQ, D), grads_in.reshape(MICRO, SEQS, SEQ, D), totals[0], totals[1], totals[2], totals[3], totals[4], totals[5], totals[6], totals[7], totals[8], totals[9], totals[10], totals[11])
```

```python
from functools import partial

import jax
import jax.numpy as jnp
from jax import lax
from jax.experimental import pallas as pl
from jax.experimental.pallas import tpu as pltpu
from jax.sharding import PartitionSpec as P

BLK = 256
CHUNK = 512
TILE = 256
HIGHEST = lax.Precision.HIGHEST
EPSILON = 1e-05
RIDGE_TERM = 0.5
SIGMA_SCALE = 0.01
MASKED = -1e30
F32 = jnp.float32
BF16 = jnp.bfloat16
VMEM_BYTES = 60 * 1024 * 1024


def dot(a, b, ca=1, cb=0):
    return lax.dot_general(a, b, (((ca,), (cb,)), ((), ())), preferred_element_type=F32)


def row_spec(shape, index):
    return pl.BlockSpec(shape, index)


def params(limit=VMEM_BYTES):
    return pltpu.CompilerParams(vmem_limit_bytes=limit)


def layer_norm(inputs, gains, offsets):
    centred = inputs - jnp.mean(inputs, axis=-1, keepdims=True)
    inv_std = lax.rsqrt(jnp.mean(centred * centred, axis=-1, keepdims=True) + EPSILON)
    normed = centred * inv_std
    return (normed * gains + offsets, normed, inv_std)


def basis_rows(sample_pos, length, basis_count):
    times = (sample_pos.astype(F32) + 0.5) / length
    centres = (jnp.arange(basis_count, dtype=F32) + 0.5) / basis_count
    width = 1.25 / basis_count
    return jnp.exp(-((times[..., None] - centres) ** 2) / (2.0 * width * width))


def inverse_kernel(a_ref, o_ref):
    count, size = a_ref.shape[0], a_ref.shape[1]
    lanes = lax.broadcasted_iota(jnp.int32, (1, size), 1)
    rows = lax.broadcasted_iota(jnp.int32, (size, 1), 0)
    for m in range(count):
        o_ref[m] = a_ref[m]

    def eliminate(k, carry):
        here = lanes == k
        for m in range(count):
            full = o_ref[m]
            row = o_ref[m, pl.ds(k, 1), :]
            pivot = jnp.sum(jnp.where(here, row, 0.0), axis=1, keepdims=True)
            column = jnp.sum(jnp.where(here, full, 0.0), axis=1, keepdims=True)
            recip = 1.0 / pivot
            scaled = jnp.where(here, recip, row * recip)
            kept = jnp.where(here, 0.0, full)
            o_ref[m] = jnp.where(rows == k, scaled, kept - column * scaled)
        return carry

    lax.fori_loop(0, size, eliminate, 0)


def spd_inverse(systems):
    return pl.pallas_call(
        inverse_kernel,
        out_shape=jax.ShapeDtypeStruct(systems.shape, F32),
        compiler_params=params(),
        cost_estimate=pl.CostEstimate(flops=20_000_000, bytes_accessed=300_000, transcendentals=0),
        name="inverse",
    )(systems)


def pick(stats, lanes, index):
    return jnp.sum(jnp.where(lanes == index, stats, 0.0), axis=1, keepdims=True)


def forward_kernel(q_ref, k_ref, v_ref, dcol_ref, drow_ref, st_ref, c_ref, p_ref, e_ref, *, ext):
    pair = pl.program_id(1)
    basis = k_ref.shape[1] - ext
    lanes = lax.broadcasted_iota(jnp.int32, (1, 128), 1)
    centres = (lax.broadcasted_iota(jnp.int32, (1, basis), 1).astype(F32) + 0.5) / basis
    mem_v = v_ref[0, ext:, :]
    for i in range(ext // BLK - 1):
        lo = i * BLK
        queries = q_ref[0, lo : lo + BLK, :] * BF16(0.125)
        keys = k_ref[0, lo : lo + 2 * BLK, :]
        vals = v_ref[0, lo : lo + 2 * BLK, :]
        allowed = dcol_ref[0, lo + BLK : lo + 2 * BLK, :] == drow_ref[0, :, lo : lo + 2 * BLK]
        stats = st_ref[0, lo : lo + BLK, :]
        mixed = []
        for half in range(2):
            head = 2 * pair + half
            mine = (lanes // 64) == half
            scores = dot(jnp.where(mine, queries, BF16(0)), keys, 1, 1)
            scores = jnp.where(allowed, scores, MASKED)
            top = jnp.max(scores, axis=1, keepdims=True)
            probs = jnp.exp(scores - top)
            probs = probs * (1.0 / jnp.sum(probs, axis=1, keepdims=True))
            probs = probs.astype(BF16)
            p_ref[0, half, i] = probs
            gap = pick(stats, lanes, head) - centres
            density = pick(stats, lanes, 32 + head) * jnp.exp(
                -(gap * gap) * pick(stats, lanes, 16 + head)
            )
            density = density.astype(BF16)
            e_ref[0, half, lo : lo + BLK, :] = density
            mixed.append(dot(probs, vals) + dot(density, mem_v))
        c_ref[0, lo : lo + BLK, :] = jnp.where(lanes < 64, mixed[0], mixed[1]).astype(BF16)


def backward_kernel(
    dc_ref, q_ref, k_ref, v_ref, p_ref, e_ref, st_ref, km_ref, ks_ref, mw_ref, sw_ref,
    dq_ref, dk_ref, dv_ref, qm_ref, dk_acc, dv_acc, *, ext
):
    pair = pl.program_id(1)
    basis = k_ref.shape[1] - ext
    lanes = lax.broadcasted_iota(jnp.int32, (1, 128), 1)
    centres = (lax.broadcasted_iota(jnp.int32, (1, basis), 1).astype(F32) + 0.5) / basis
    mem_v = v_ref[0, ext:, :]
    dk_acc[...] = jnp.zeros_like(dk_acc)
    dv_acc[...] = jnp.zeros_like(dv_acc)
    km, ks = km_ref[0], ks_ref[0]
    sum_m = jnp.zeros((1, 128), F32)
    sum_s = jnp.zeros((1, 128), F32)
    for i in range(ext // BLK - 1):
        lo = i * BLK
        raw = q_ref[0, lo : lo + BLK, :]
        queries = raw * BF16(0.125)
        keys = k_ref[0, lo : lo + 2 * BLK, :]
        vals = v_ref[0, lo : lo + 2 * BLK, :]
        grads = dc_ref[0, lo : lo + BLK, :]
        stats = st_ref[0, lo : lo + BLK, :]
        dq_parts, dm_parts, dsp_parts = [], [], []
        for half in range(2):
            head = 2 * pair + half
            mine = (lanes // 64) == half
            own_grad = jnp.where(mine, grads, BF16(0))
            own_q = jnp.where(mine, queries, BF16(0))
            probs = p_ref[0, half, i]
            wide = probs.astype(F32)
            prod = wide * dot(own_grad, vals, 1, 1)
            total = jnp.sum(prod, axis=1, keepdims=True)
            dscore = (prod - wide * total).astype(BF16)
            dq_parts.append(dot(dscore, keys))
            dk_acc[lo : lo + 2 * BLK, :] += dot(dscore, own_q, 0, 0)
            dv_acc[lo : lo + 2 * BLK, :] += dot(probs, own_grad, 0, 0)
            density = e_ref[0, half, lo : lo + BLK, :]
            dv_acc[ext:, :] += dot(density, own_grad, 0, 0)
            weight = density.astype(F32) * dot(own_grad, mem_v, 1, 1)
            gap = pick(stats, lanes, head) - centres
            first = weight * gap
            s_zero = jnp.sum(weight, axis=1, keepdims=True)
            s_one = jnp.sum(first, axis=1, keepdims=True)
            s_two = jnp.sum(first * gap, axis=1, keepdims=True)
            dm_parts.append(s_one * pick(stats, lanes, 48 + head))
            dsp_parts.append(
                s_two * pick(stats, lanes, 64 + head) + s_zero * pick(stats, lanes, 80 + head)
            )
        low = lanes < 64
        d_mean = jnp.where(low, dm_parts[0], dm_parts[1])
        d_spread = jnp.where(low, dsp_parts[0], dsp_parts[1])
        dq = jnp.where(low, dq_parts[0], dq_parts[1]) * 0.125 + d_mean * km + d_spread * ks
        dq_ref[0, lo : lo + BLK, :] = dq.astype(BF16)
        wide_q = raw.astype(F32)
        sum_m += jnp.sum(d_mean * wide_q, axis=0, keepdims=True)
        sum_s += jnp.sum(d_spread * wide_q, axis=0, keepdims=True)
    dk_ref[0, :ext, :] = dk_acc[:ext, :].astype(BF16)
    dk_ref[0, ext:, :] = (0.125 * (mw_ref[...] * sum_m + sw_ref[...] * sum_s)).astype(BF16)
    dv_ref[0] = dv_acc[...].astype(BF16)
    rows = lax.broadcasted_iota(jnp.int32, (8, 1), 0)
    qm_ref[0] = jnp.where(rows == 0, sum_m, jnp.where(rows == 1, sum_s, 0.0))


def middle_kernel(
    x_ref, cot_ref, c_ref, wout_ref, wfc_ref, wproj_ref, vec_ref, fcb_ref,
    out_ref, dr_ref, dc_ref, dwout_ref, dwfc_ref, dwproj_ref, dfcb_ref, vecg_ref,
    r_s, h_s, y_s, g_s, act_s, du_s, do_s
):
    chunk = pl.program_id(0)
    tiles = x_ref.shape[0] // TILE
    gain, bias, out_bias = vec_ref[0:1, :], vec_ref[1:2, :], vec_ref[2:3, :]

    def rows_of(t):
        return pl.ds(pl.multiple_of(t * TILE, TILE), TILE)

    @pl.when(chunk == 0)
    def _():
        def start(t, carry):
            rows = rows_of(t)
            resid = x_ref[rows, :].astype(F32) + dot(c_ref[rows, :], wout_ref[...])
            r_s[rows, :] = resid
            h_s[rows, :] = layer_norm(resid, gain, bias)[0].astype(BF16)
            y_s[rows, :] = resid + out_bias
            g_s[rows, :] = jnp.zeros((TILE, g_s.shape[1]), F32)
            return carry

        lax.fori_loop(0, tiles, start, 0)

    wfc, wproj, fcb = wfc_ref[...], wproj_ref[...], fcb_ref[0]

    def body(t, sums):
        rows = rows_of(t)
        pre = dot(h_s[rows, :], wfc) + fcb
        sq = pre * pre
        th = jnp.tanh(pre * (0.7978845608028654 + 0.035677408136300125 * sq))
        half = 0.5 * (1.0 + th)
        act = (pre * half).astype(BF16)
        slope = half + 0.5 * pre * (1.0 - th * th) * (
            0.7978845608028654 + 0.10703222440890037 * sq
        )
        act_s[rows, :] = act
        y_s[rows, :] += dot(act, wproj)
        du = (dot(cot_ref[rows, :], wproj, 1, 1) * slope).astype(BF16)
        du_s[rows, :] = du
        g_s[rows, :] += dot(du, wfc, 1, 1)
        return sums + jnp.sum(du.astype(F32), axis=0, keepdims=True)

    dfcb_ref[0] = lax.fori_loop(0, tiles, body, jnp.zeros((1, CHUNK), F32))
    dwproj_ref[...] = dot(act_s[...], cot_ref[...], 0, 0).astype(BF16)
    dwfc = dot(h_s[...], du_s[...], 0, 0).astype(BF16)
    share = dwfc_ref.shape[2]
    for f in range(dwfc_ref.shape[0]):
        dwfc_ref[f, 0] = dwfc[f * share : (f + 1) * share, :]

    @pl.when(chunk == pl.num_programs(0) - 1)
    def _():
        def finish(t, sums):
            rows = rows_of(t)
            out_ref[rows, :] = y_s[rows, :].astype(BF16)
            cot = cot_ref[rows, :].astype(F32)
            grad = g_s[rows, :]
            _, normed, inv_std = layer_norm(r_s[rows, :], gain, bias)
            gnorm = grad * gain
            resid = cot + inv_std * (
                gnorm
                - jnp.mean(gnorm, axis=-1, keepdims=True)
                - normed * jnp.mean(gnorm * normed, axis=-1, keepdims=True)
            )
            dr_ref[rows, :] = resid
            branch = resid.astype(BF16)
            do_s[rows, :] = branch
            dc_ref[rows, :] = dot(branch, wout_ref[...], 1, 1).astype(BF16)
            return (
                sums[0] + jnp.sum(grad * normed, axis=0, keepdims=True),
                sums[1] + jnp.sum(grad, axis=0, keepdims=True),
                sums[2] + jnp.sum(cot, axis=0, keepdims=True),
            )

        zero = jnp.zeros((1, x_ref.shape[1]), F32)
        sums = lax.fori_loop(0, tiles, finish, (zero, zero, zero))
        index = lax.broadcasted_iota(jnp.int32, (8, 1), 0)
        vecg_ref[...] = jnp.where(
            index == 0,
            sums[0],
            jnp.where(index == 1, sums[1], jnp.where(index == 2, sums[2], 0.0)),
        )
        dwout_ref[...] = dot(c_ref[...], do_s[...], 0, 0).astype(BF16)


def middle(x, cot, ctx, w_out, w_fc, w_proj, vecs, fc_bias, group):
    rows, dim = x.shape
    hidden = w_fc.shape[1]
    steps = hidden // CHUNK
    share = dim // group

    def fixed(shape):
        return pl.BlockSpec(shape, lambda c: (0,) * len(shape), pipeline_mode=pl.Buffered(1))

    return pl.pallas_call(
        middle_kernel,
        grid=(steps,),
        in_specs=[
            fixed((rows, dim)),
            fixed((rows, dim)),
            fixed((rows, dim)),
            fixed((dim, dim)),
            pl.BlockSpec((dim, CHUNK), lambda c: (0, c)),
            pl.BlockSpec((CHUNK, dim), lambda c: (c, 0)),
            fixed((8, dim)),
            pl.BlockSpec((1, 1, CHUNK), lambda c: (c, 0, 0)),
        ],
        out_specs=[
            fixed((rows, dim)),
            fixed((rows, dim)),
            fixed((rows, dim)),
            fixed((dim, dim)),
            pl.BlockSpec((group, 1, share, CHUNK), lambda c: (0, c, 0, 0)),
            pl.BlockSpec((CHUNK, dim), lambda c: (c, 0)),
            pl.BlockSpec((1, 1, CHUNK), lambda c: (c, 0, 0)),
            fixed((8, dim)),
        ],
        out_shape=[
            jax.ShapeDtypeStruct((rows, dim), BF16),
            jax.ShapeDtypeStruct((rows, dim), F32),
            jax.ShapeDtypeStruct((rows, dim), BF16),
            jax.ShapeDtypeStruct((dim, dim), BF16),
            jax.ShapeDtypeStruct((group, steps, share, CHUNK), BF16),
            jax.ShapeDtypeStruct((hidden, dim), BF16),
            jax.ShapeDtypeStruct((steps, 1, CHUNK), F32),
            jax.ShapeDtypeStruct((8, dim), F32),
        ],
        scratch_shapes=[
            pltpu.VMEM((rows, dim), F32),
            pltpu.VMEM((rows, dim), BF16),
            pltpu.VMEM((rows, dim), F32),
            pltpu.VMEM((rows, dim), F32),
            pltpu.VMEM((rows, CHUNK), BF16),
            pltpu.VMEM((rows, CHUNK), BF16),
            pltpu.VMEM((rows, dim), BF16),
        ],
        compiler_params=params(),
        cost_estimate=pl.CostEstimate(
            flops=12 * rows * dim * hidden, bytes_accessed=40_000_000, transcendentals=0
        ),
        name="middle",
    )(x, cot, ctx, w_out, w_fc, w_proj, vecs, fc_bias)


def attend(q, kv, dcol, drow, stats, ext):
    micro, tok, dim = q.shape
    total = kv.shape[1]
    pairs = dim // 128
    blocks = tok // BLK
    return pl.pallas_call(
        partial(forward_kernel, ext=ext),
        grid=(micro, pairs),
        in_specs=[
            pl.BlockSpec((1, tok, 128), lambda m, p: (m, 0, p)),
            pl.BlockSpec((1, total, 128), lambda m, p: (m, 0, p)),
            pl.BlockSpec((1, total, 128), lambda m, p: (m, 0, pairs + p)),
            pl.BlockSpec((1, ext, 1), lambda m, p: (m, 0, 0)),
            pl.BlockSpec((1, 1, ext), lambda m, p: (m, 0, 0)),
            pl.BlockSpec((1, tok, 128), lambda m, p: (m, 0, 0)),
        ],
        out_specs=[
            pl.BlockSpec((1, tok, 128), lambda m, p: (m, 0, p)),
            pl.BlockSpec((1, 2, blocks, BLK, 2 * BLK), lambda m, p: (m, p, 0, 0, 0)),
            pl.BlockSpec((1, 2, tok, total - ext), lambda m, p: (m, p, 0, 0)),
        ],
        out_shape=[
            jax.ShapeDtypeStruct((micro, tok, dim), BF16),
            jax.ShapeDtypeStruct((micro, 2 * pairs, blocks, BLK, 2 * BLK), BF16),
            jax.ShapeDtypeStruct((micro, 2 * pairs, tok, total - ext), BF16),
        ],
        compiler_params=params(),
        cost_estimate=pl.CostEstimate(
            flops=8 * micro * tok * 768 * dim, bytes_accessed=30_000_000, transcendentals=0
        ),
        name="attend",
    )(q, kv, kv, dcol, drow, stats)


def attend_back(dctx, q, kv, probs, density, stats, km, ks, mean_wide, spread_wide, ext):
    micro, tok, dim = q.shape
    total = kv.shape[1]
    pairs = dim // 128
    blocks = tok // BLK
    basis = total - ext
    part = pl.BlockSpec((1, tok, 128), lambda m, p: (m, 0, p))
    rows = pl.BlockSpec((1, total, 128), lambda m, p: (m, 0, p))
    line = pl.BlockSpec((1, 1, 128), lambda m, p: (m, 0, p))
    wide = pl.BlockSpec((basis, 128), lambda m, p: (0, p))
    return pl.pallas_call(
        partial(backward_kernel, ext=ext),
        grid=(micro, pairs),
        in_specs=[
            part,
            part,
            rows,
            pl.BlockSpec((1, total, 128), lambda m, p: (m, 0, pairs + p)),
            pl.BlockSpec((1, 2, blocks, BLK, 2 * BLK), lambda m, p: (m, p, 0, 0, 0)),
            pl.BlockSpec((1, 2, tok, basis), lambda m, p: (m, p, 0, 0)),
            pl.BlockSpec((1, tok, 128), lambda m, p: (m, 0, 0)),
            line,
            line,
            wide,
            wide,
        ],
        out_specs=[part, rows, rows, pl.BlockSpec((1, 8, 128), lambda m, p: (m, 0, p))],
        out_shape=[
            jax.ShapeDtypeStruct((micro, tok, dim), BF16),
            jax.ShapeDtypeStruct((micro, total, dim), BF16),
            jax.ShapeDtypeStruct((micro, total, dim), BF16),
            jax.ShapeDtypeStruct((micro, 8, dim), F32),
        ],
        scratch_shapes=[pltpu.VMEM((total, 128), F32), pltpu.VMEM((total, 128), F32)],
        compiler_params=params(),
        cost_estimate=pl.CostEstimate(
            flops=16 * micro * tok * 768 * dim, bytes_accessed=30_000_000, transcendentals=0
        ),
        name="attend_back",
    )(dctx, q, kv, kv, probs, density, stats, km, ks, mean_wide, spread_wide)


def on_device(
    tokens,
    cotangent,
    doc_ids,
    positions,
    w_qkv,
    w_out,
    w_fc,
    w_proj,
    ln1_gain,
    ln1_bias,
    ln2_gain,
    ln2_bias,
    fc_bias,
    proj_bias,
    mean_weight,
    spread_weight,
):
    group = lax.axis_size("fsdp")
    member = lax.axis_index("fsdp")
    micro, tok, dim = tokens.shape[0], tokens.shape[2], tokens.shape[3]
    hidden = w_fc.shape[1]
    heads = mean_weight.shape[1]
    basis = mean_weight.shape[0] * group
    head_dim = dim // heads
    seq_len = tok * group
    own_count = positions.shape[2] // group
    first_row = member * tok
    ext = tok + BLK
    x = tokens[:, 0]
    cot = cotangent[:, 0]

    onward = [(i, i + 1) for i in range(group - 1)]
    edge = lax.ppermute(x[:, tok - BLK :], "fsdp", onward)
    sample_pos = positions[:, 0]
    own_rows = lax.dynamic_slice_in_dim(sample_pos, member * own_count, own_count, 1) - first_row
    hot = (own_rows[:, :, None] == jnp.arange(tok)[None, None, :]).astype(BF16)
    picked = jnp.einsum("mst,mtd->msd", hot, x, preferred_element_type=F32).astype(BF16)
    picked = lax.all_gather(picked, "fsdp", axis=1, tiled=True)

    small = [ln1_gain, ln1_bias, ln2_gain, ln2_bias, fc_bias, proj_bias]
    small = small + [mean_weight.reshape(-1), spread_weight.reshape(-1)]
    packed = lax.all_gather(jnp.concatenate(small), "fsdp", axis=0, tiled=False)
    vectors, at = [], 0
    for piece in small:
        vectors.append(packed[:, at : at + piece.shape[0]].reshape(-1).astype(F32))
        at = at + piece.shape[0]
    gain_one, bias_one, gain_two, bias_two, hidden_bias, output_bias = vectors[:6]
    mean_f32 = vectors[6].reshape(basis, heads)
    spread_f32 = vectors[7].reshape(basis, heads)
    full_qkv, full_out, full_fc, full_proj = (
        lax.all_gather(w, "fsdp", axis=0, tiled=True) for w in (w_qkv, w_out, w_fc, w_proj)
    )

    table = basis_rows(sample_pos, seq_len, basis)
    if sample_pos.shape[1] < basis:
        system = jnp.einsum("msn,mtn->mst", table, table, precision=HIGHEST)
        system = system + RIDGE_TERM * jnp.eye(sample_pos.shape[1], dtype=F32)
        solver = jnp.einsum("msn,mst->mnt", table, spd_inverse(system), precision=HIGHEST)
    else:
        system = jnp.einsum("msn,msk->mnk", table, table, precision=HIGHEST)
        system = system + RIDGE_TERM * jnp.eye(basis, dtype=F32)
        solver = jnp.einsum("mkn,msn->mks", spd_inverse(system), table, precision=HIGHEST)

    inputs = x.astype(F32)
    own_low = layer_norm(inputs, gain_one, bias_one)[0].astype(BF16)
    edge_low = layer_norm(edge.astype(F32), gain_one, bias_one)[0].astype(BF16)
    picked_low = layer_norm(picked.astype(F32), gain_one, bias_one)[0].astype(BF16)
    coeff = jnp.einsum("mns,msd->mnd", solver, picked_low.astype(F32), precision=HIGHEST)
    rows_low = jnp.concatenate([edge_low, own_low, coeff.astype(BF16)], axis=1)
    q = jnp.einsum(
        "mtd,de->mte", own_low, full_qkv[:, :dim], preferred_element_type=F32
    ).astype(BF16)
    kv = jnp.einsum(
        "mtd,de->mte", rows_low, full_qkv[:, dim:], preferred_element_type=F32
    ).astype(BF16)

    mean_wide = jnp.repeat(mean_f32, head_dim, axis=1)
    spread_wide = jnp.repeat(spread_f32, head_dim, axis=1)
    mem_keys = kv[:, ext:, :dim].astype(F32)
    km = jnp.sum(mem_keys * mean_wide, axis=1) * head_dim ** (-0.5)
    ks = jnp.sum(mem_keys * spread_wide, axis=1) * head_dim ** (-0.5)
    owner = (jnp.arange(dim)[:, None] // head_dim == jnp.arange(heads)[None, :]).astype(F32)
    both = jnp.concatenate([km[:, :, None] * owner, ks[:, :, None] * owner], axis=2)
    logits = jnp.einsum("mtd,mdj->mtj", q.astype(F32), both, precision=HIGHEST)
    middle_at = jax.nn.sigmoid(logits[:, :, :heads])
    basis_var = (1.25 / basis) ** 2
    spread_logit = logits[:, :, heads:]
    spread_sq = basis_var + SIGMA_SCALE * jax.nn.softplus(spread_logit)
    inv_two = 0.5 / spread_sq
    spread_slope = SIGMA_SCALE * jax.nn.sigmoid(spread_logit)
    columns = [
        middle_at,
        inv_two,
        jnp.sqrt(basis_var / spread_sq),
        -2.0 * inv_two * middle_at * (1.0 - middle_at),
        2.0 * inv_two * inv_two * spread_slope,
        -inv_two * spread_slope,
    ]
    stats = jnp.concatenate(
        [jnp.pad(c, ((0, 0), (0, 0), (0, 16 - heads))) for c in columns]
        + [jnp.zeros((micro, tok, 32), F32)],
        axis=2,
    )

    padded = jnp.concatenate([jnp.full((micro, BLK), -1, jnp.int32), doc_ids[:, 0]], axis=1)
    ext_docs = lax.dynamic_slice_in_dim(padded, first_row, ext, 1)
    ctx, probs, density = attend(
        q, kv, ext_docs[:, :, None], ext_docs[:, None, :], stats, ext
    )

    vecs = jnp.concatenate(
        [v[None] for v in (gain_two, bias_two, output_bias)] + [jnp.zeros((5, dim), F32)]
    )
    rows = micro * tok
    output, d_resid, d_ctx, dw_out, dw_fc, dw_proj, d_hidden, d_vecs = middle(
        x.reshape(rows, dim),
        cot.reshape(rows, dim),
        ctx.reshape(rows, dim),
        full_out,
        full_fc,
        full_proj,
        vecs,
        hidden_bias.reshape(-1, 1, CHUNK),
        group,
    )

    both_axes = ("fsdp", "rep")

    def reduced(parts):
        own = lax.psum_scatter(parts, both_axes, scatter_dimension=0, tiled=True)
        return lax.all_gather(own, "rep", axis=0, tiled=True)

    sum_proj = reduced(dw_proj)
    sum_fc = reduced(dw_fc.reshape(-1, CHUNK))

    d_q, d_k, d_v, d_sums = attend_back(
        d_ctx.reshape(micro, tok, dim),
        q,
        kv,
        probs,
        density,
        stats,
        km[:, None],
        ks[:, None],
        mean_wide,
        spread_wide,
        ext,
    )
    mean_term = jnp.sum(mem_keys * d_sums[:, 0:1], axis=0) * head_dim ** (-0.5)
    spread_term = jnp.sum(mem_keys * d_sums[:, 1:2], axis=0) * head_dim ** (-0.5)
    acc_mean = jnp.dot(mean_term, owner, precision=HIGHEST)
    acc_spread = jnp.dot(spread_term, owner, precision=HIGHEST)

    def back(grad, low, high):
        return jnp.einsum(
            "mte,de->mtd", grad, full_qkv[:, low:high], preferred_element_type=F32
        )

    d_rows = back(d_k, dim, 2 * dim) + back(d_v, 2 * dim, 3 * dim)
    returned = lax.ppermute(
        d_rows[:, :BLK].astype(BF16), "fsdp", [(i + 1, i) for i in range(group - 1)]
    )
    d_picked = jnp.einsum("mns,mnd->msd", solver, d_rows[:, ext:], precision=HIGHEST)
    d_picked = lax.psum_scatter(
        d_picked.astype(BF16), "fsdp", scatter_dimension=1, tiled=True
    )

    def flat(value):
        return value.reshape(-1, value.shape[-1])

    dw_q = dot(flat(own_low), flat(d_q), 0, 0).astype(BF16)
    dw_k = dot(flat(rows_low), flat(d_k), 0, 0).astype(BF16)
    dw_v = dot(flat(rows_low), flat(d_v), 0, 0).astype(BF16)
    last = jnp.stack([v.reshape(group, -1, dim) for v in (dw_out, dw_q, dw_k, dw_v)], axis=1)
    sum_last = reduced(last.reshape(-1, dim)).reshape(4, -1, dim)

    d_first = d_rows[:, BLK:ext] + back(d_q, 0, dim)
    d_first = d_first + jnp.einsum("mst,msd->mtd", hot, d_picked, preferred_element_type=F32)
    d_first = d_first + jnp.pad(returned.astype(F32), ((0, 0), (tok - BLK, 0), (0, 0)))
    _, normed, inv_std = layer_norm(inputs, gain_one, bias_one)
    g_norm = d_first * gain_one
    grad_tokens = d_resid.reshape(micro, tok, dim) + inv_std * (
        g_norm
        - jnp.mean(g_norm, axis=-1, keepdims=True)
        - normed * jnp.mean(g_norm * normed, axis=-1, keepdims=True)
    )
    acc_gain_one = jnp.sum(d_first * normed, axis=(0, 1))
    acc_bias_one = jnp.sum(d_first, axis=(0, 1))

    vector_parts = [
        acc_gain_one,
        acc_bias_one,
        d_vecs[0],
        d_vecs[1],
        d_hidden,
        d_vecs[2],
        acc_mean,
        acc_spread,
    ]
    joined = jnp.concatenate([v.reshape(group, -1) for v in vector_parts], axis=1)
    joined = lax.psum(joined, both_axes)
    own = lax.dynamic_slice_in_dim(joined, member, 1, 0)[0]
    pieces, at = [], 0
    for part in vector_parts:
        size = part.size // group
        pieces.append(own[at : at + size])
        at = at + size
    share = dim // group
    grad_fc = sum_fc.reshape(hidden // CHUNK, share, CHUNK).transpose(1, 0, 2)
    grad_qkv = jnp.concatenate([sum_last[1], sum_last[2], sum_last[3]], axis=1)
    return (
        output.reshape(micro, 1, tok, dim),
        grad_tokens[:, None],
        grad_qkv.astype(F32),
        sum_last[0].astype(F32),
        grad_fc.reshape(share, hidden).astype(F32),
        sum_proj.astype(F32),
        pieces[0],
        pieces[1],
        pieces[2],
        pieces[3],
        pieces[4],
        pieces[5],
        pieces[6].reshape(-1, heads),
        pieces[7].reshape(-1, heads),
    )


def solution(mesh):
    seq = P(None, "rep", "fsdp", None)
    row = P("fsdp", None)
    vec = P("fsdp")
    return jax.shard_map(
        on_device,
        mesh=mesh,
        in_specs=(seq, seq, P(None, "rep", None), P(None, "rep", None))
        + (row, row, row, row)
        + (vec,) * 6
        + (row, row),
        out_specs=(seq, seq, row, row, row, row) + (vec,) * 6 + (row, row),
        check_vma=False,
    )
```

```python
from functools import partial

import jax
import jax.numpy as jnp
from jax import lax
from jax.experimental import pallas as pl
from jax.experimental.pallas import tpu as pltpu
from jax.sharding import PartitionSpec as P

BLK = 256
CHUNK = 512
TILE = 256
HIGHEST = lax.Precision.HIGHEST
EPSILON = 1e-05
RIDGE_TERM = 0.5
SIGMA_SCALE = 0.01
MASKED = -1e30
F32 = jnp.float32
BF16 = jnp.bfloat16
VMEM_BYTES = 60 * 1024 * 1024


def dot(a, b, ca=1, cb=0):
    return lax.dot_general(a, b, (((ca,), (cb,)), ((), ())), preferred_element_type=F32)


def row_spec(shape, index):
    return pl.BlockSpec(shape, index)


def params(limit=VMEM_BYTES):
    return pltpu.CompilerParams(vmem_limit_bytes=limit)


def bits_of(axis):
    return range(lax.axis_size(axis).bit_length() - 1)


def side(axis, bit):
    return (lax.axis_index(axis) >> bit) & 1


def swapped(value, axis, bit):
    return lax.ppermute(value, axis, [(i, i ^ (1 << bit)) for i in range(lax.axis_size(axis))])


def halved(value, axis, bit, dim):
    half = value.shape[dim] // 2
    mine = side(axis, bit)
    kept = lax.dynamic_slice_in_dim(value, mine * half, half, dim)
    sent = lax.dynamic_slice_in_dim(value, (1 - mine) * half, half, dim)
    return kept + swapped(sent, axis, bit)


def doubled(value, other, mine, dim):
    return jnp.where(
        mine == 0,
        jnp.concatenate([value, other], axis=dim),
        jnp.concatenate([other, value], axis=dim),
    )


def gathered(value, axis, dim):
    for bit in bits_of(axis):
        value = doubled(value, swapped(value, axis, bit), side(axis, bit), dim)
    return value


def scattered(value, axis, dim):
    for bit in reversed(bits_of(axis)):
        value = halved(value, axis, bit, dim)
    return value


def gathered_weight(weight):
    if lax.axis_size("fsdp") != 2:
        return lax.all_gather(weight, "fsdp", axis=0, tiled=True)
    core = side("rep", 0)
    half = weight.shape[0] // 2
    sent = lax.dynamic_slice_in_dim(weight, core * half, half, 0)
    first = swapped(sent, "fsdp", 0)
    other = doubled(first, swapped(first, "rep", 0), core, 0)
    return doubled(weight, other, side("fsdp", 0), 0)


def reduced(parts, early):
    own = halved(parts, "rep", 0, 1)
    order = list(bits_of("rep"))[1:]
    for bit in order[:early]:
        own = halved(own, "rep", bit, 1)
    own = scattered(own, "fsdp", 0)
    for bit in order[early:]:
        own = halved(own, "rep", bit, 1)
    own = own[0]
    for bit in reversed(bits_of("rep")):
        own = doubled(own, swapped(own, "rep", bit), side("rep", bit), 0)
    return own


def layer_norm(inputs, gains, offsets):
    centred = inputs - jnp.mean(inputs, axis=-1, keepdims=True)
    inv_std = lax.rsqrt(jnp.mean(centred * centred, axis=-1, keepdims=True) + EPSILON)
    normed = centred * inv_std
    return (normed * gains + offsets, normed, inv_std)


def basis_rows(sample_pos, length, basis_count):
    times = (sample_pos.astype(F32) + 0.5) / length
    centres = (jnp.arange(basis_count, dtype=F32) + 0.5) / basis_count
    width = 1.25 / basis_count
    return jnp.exp(-((times[..., None] - centres) ** 2) / (2.0 * width * width))


def inverse_kernel(a_ref, o_ref):
    count, size = a_ref.shape[0], a_ref.shape[1]
    lanes = lax.broadcasted_iota(jnp.int32, (1, size), 1)
    rows = lax.broadcasted_iota(jnp.int32, (size, 1), 0)
    for m in range(count):
        o_ref[m] = a_ref[m]

    def eliminate(k, carry):
        here = lanes == k
        for m in range(count):
            full = o_ref[m]
            row = o_ref[m, pl.ds(k, 1), :]
            pivot = jnp.sum(jnp.where(here, row, 0.0), axis=1, keepdims=True)
            column = jnp.sum(jnp.where(here, full, 0.0), axis=1, keepdims=True)
            recip = 1.0 / pivot
            scaled = jnp.where(here, recip, row * recip)
            kept = jnp.where(here, 0.0, full)
            o_ref[m] = jnp.where(rows == k, scaled, kept - column * scaled)
        return carry

    lax.fori_loop(0, size, eliminate, 0)


def spd_inverse(systems):
    return pl.pallas_call(
        inverse_kernel,
        out_shape=jax.ShapeDtypeStruct(systems.shape, F32),
        compiler_params=params(),
        cost_estimate=pl.CostEstimate(flops=26_000_000_000, bytes_accessed=300_000, transcendentals=0),
        name="inverse",
    )(systems)


def pick(stats, lanes, index):
    return jnp.sum(jnp.where(lanes == index, stats, 0.0), axis=1, keepdims=True)


def forward_kernel(q_ref, k_ref, v_ref, dcol_ref, drow_ref, st_ref, c_ref, p_ref, e_ref, *, ext):
    pair = pl.program_id(1)
    basis = k_ref.shape[1] - ext
    lanes = lax.broadcasted_iota(jnp.int32, (1, 128), 1)
    centres = (lax.broadcasted_iota(jnp.int32, (1, basis), 1).astype(F32) + 0.5) / basis
    mem_v = v_ref[0, ext:, :]
    for i in range(ext // BLK - 1):
        lo = i * BLK
        queries = q_ref[0, lo : lo + BLK, :] * BF16(0.125)
        keys = k_ref[0, lo : lo + 2 * BLK, :]
        vals = v_ref[0, lo : lo + 2 * BLK, :]
        allowed = dcol_ref[0, lo + BLK : lo + 2 * BLK, :] == drow_ref[0, :, lo : lo + 2 * BLK]
        stats = st_ref[0, lo : lo + BLK, :]
        mixed = []
        for half in range(2):
            head = 2 * pair + half
            mine = (lanes // 64) == half
            scores = dot(jnp.where(mine, queries, BF16(0)), keys, 1, 1)
            scores = jnp.where(allowed, scores, MASKED)
            top = jnp.max(scores, axis=1, keepdims=True)
            probs = jnp.exp(scores - top)
            probs = probs * (1.0 / jnp.sum(probs, axis=1, keepdims=True))
            probs = probs.astype(BF16)
            p_ref[0, half, i] = probs
            gap = pick(stats, lanes, head) - centres
            density = pick(stats, lanes, 32 + head) * jnp.exp(
                -(gap * gap) * pick(stats, lanes, 16 + head)
            )
            density = density.astype(BF16)
            e_ref[0, half, lo : lo + BLK, :] = density
            mixed.append(dot(probs, vals) + dot(density, mem_v))
        c_ref[0, lo : lo + BLK, :] = jnp.where(lanes < 64, mixed[0], mixed[1]).astype(BF16)


def backward_kernel(
    dc_ref, q_ref, k_ref, v_ref, p_ref, e_ref, st_ref, km_ref, ks_ref, mw_ref, sw_ref,
    dq_ref, dk_ref, dv_ref, qm_ref, dk_acc, dv_acc, *, ext
):
    pair = pl.program_id(1)
    basis = k_ref.shape[1] - ext
    lanes = lax.broadcasted_iota(jnp.int32, (1, 128), 1)
    centres = (lax.broadcasted_iota(jnp.int32, (1, basis), 1).astype(F32) + 0.5) / basis
    mem_v = v_ref[0, ext:, :]
    dk_acc[...] = jnp.zeros_like(dk_acc)
    dv_acc[...] = jnp.zeros_like(dv_acc)
    km, ks = km_ref[0], ks_ref[0]
    sum_m = jnp.zeros((1, 128), F32)
    sum_s = jnp.zeros((1, 128), F32)
    for i in range(ext // BLK - 1):
        lo = i * BLK
        raw = q_ref[0, lo : lo + BLK, :]
        queries = raw * BF16(0.125)
        keys = k_ref[0, lo : lo + 2 * BLK, :]
        vals = v_ref[0, lo : lo + 2 * BLK, :]
        grads = dc_ref[0, lo : lo + BLK, :]
        stats = st_ref[0, lo : lo + BLK, :]
        dq_parts, dm_parts, dsp_parts = [], [], []
        for half in range(2):
            head = 2 * pair + half
            mine = (lanes // 64) == half
            own_grad = jnp.where(mine, grads, BF16(0))
            own_q = jnp.where(mine, queries, BF16(0))
            probs = p_ref[0, half, i]
            wide = probs.astype(F32)
            prod = wide * dot(own_grad, vals, 1, 1)
            total = jnp.sum(prod, axis=1, keepdims=True)
            dscore = (prod - wide * total).astype(BF16)
            dq_parts.append(dot(dscore, keys))
            dk_acc[lo : lo + 2 * BLK, :] += dot(dscore, own_q, 0, 0)
            dv_acc[lo : lo + 2 * BLK, :] += dot(probs, own_grad, 0, 0)
            density = e_ref[0, half, lo : lo + BLK, :]
            dv_acc[ext:, :] += dot(density, own_grad, 0, 0)
            weight = density.astype(F32) * dot(own_grad, mem_v, 1, 1)
            gap = pick(stats, lanes, head) - centres
            first = weight * gap
            s_zero = jnp.sum(weight, axis=1, keepdims=True)
            s_one = jnp.sum(first, axis=1, keepdims=True)
            s_two = jnp.sum(first * gap, axis=1, keepdims=True)
            dm_parts.append(s_one * pick(stats, lanes, 48 + head))
            dsp_parts.append(
                s_two * pick(stats, lanes, 64 + head) + s_zero * pick(stats, lanes, 80 + head)
            )
        low = lanes < 64
        d_mean = jnp.where(low, dm_parts[0], dm_parts[1])
        d_spread = jnp.where(low, dsp_parts[0], dsp_parts[1])
        dq = jnp.where(low, dq_parts[0], dq_parts[1]) * 0.125 + d_mean * km + d_spread * ks
        dq_ref[0, lo : lo + BLK, :] = dq.astype(BF16)
        wide_q = raw.astype(F32)
        sum_m += jnp.sum(d_mean * wide_q, axis=0, keepdims=True)
        sum_s += jnp.sum(d_spread * wide_q, axis=0, keepdims=True)
    dk_ref[0, :ext, :] = dk_acc[:ext, :].astype(BF16)
    dk_ref[0, ext:, :] = (0.125 * (mw_ref[...] * sum_m + sw_ref[...] * sum_s)).astype(BF16)
    dv_ref[0] = dv_acc[...].astype(BF16)
    rows = lax.broadcasted_iota(jnp.int32, (8, 1), 0)
    qm_ref[0] = jnp.where(rows == 0, sum_m, jnp.where(rows == 1, sum_s, 0.0))


def middle_kernel(
    x_ref, cot_ref, c_ref, wout_ref, wfc_ref, wproj_ref, vec_ref, fcb_ref,
    out_ref, dr_ref, dc_ref, dwout_ref, dwfc_ref, dwproj_ref, dfcb_ref, vecg_ref,
    r_s, h_s, y_s, g_s, act_s, du_s, do_s
):
    chunk = pl.program_id(0)
    tiles = x_ref.shape[0] // TILE
    gain, bias, out_bias = vec_ref[0:1, :], vec_ref[1:2, :], vec_ref[2:3, :]

    def rows_of(t):
        return pl.ds(pl.multiple_of(t * TILE, TILE), TILE)

    @pl.when(chunk == 0)
    def _():
        def start(t, carry):
            rows = rows_of(t)
            resid = x_ref[rows, :].astype(F32) + dot(c_ref[rows, :], wout_ref[...])
            r_s[rows, :] = resid
            h_s[rows, :] = layer_norm(resid, gain, bias)[0].astype(BF16)
            y_s[rows, :] = resid + out_bias
            g_s[rows, :] = jnp.zeros((TILE, g_s.shape[1]), F32)
            return carry

        lax.fori_loop(0, tiles, start, 0)

    wfc, wproj, fcb = wfc_ref[...], wproj_ref[...], fcb_ref[0]

    def body(t, sums):
        rows = rows_of(t)
        pre = dot(h_s[rows, :], wfc) + fcb
        sq = pre * pre
        th = jnp.tanh(pre * (0.7978845608028654 + 0.035677408136300125 * sq))
        half = 0.5 * (1.0 + th)
        act = (pre * half).astype(BF16)
        slope = half + 0.5 * pre * (1.0 - th * th) * (
            0.7978845608028654 + 0.10703222440890037 * sq
        )
        act_s[rows, :] = act
        y_s[rows, :] += dot(act, wproj)
        du = (dot(cot_ref[rows, :], wproj, 1, 1) * slope).astype(BF16)
        du_s[rows, :] = du
        g_s[rows, :] += dot(du, wfc, 1, 1)
        return sums + jnp.sum(du.astype(F32), axis=0, keepdims=True)

    dfcb_ref[0] = lax.fori_loop(0, tiles, body, jnp.zeros((1, CHUNK), F32))
    dwproj_ref[...] = dot(act_s[...], cot_ref[...], 0, 0).astype(BF16)
    dwfc = dot(h_s[...], du_s[...], 0, 0).astype(BF16)
    share = dwfc_ref.shape[2]
    for f in range(dwfc_ref.shape[0]):
        dwfc_ref[f, 0] = dwfc[f * share : (f + 1) * share, :]

    @pl.when(chunk == pl.num_programs(0) - 1)
    def _():
        def finish(t, sums):
            rows = rows_of(t)
            out_ref[rows, :] = y_s[rows, :].astype(BF16)
            cot = cot_ref[rows, :].astype(F32)
            grad = g_s[rows, :]
            _, normed, inv_std = layer_norm(r_s[rows, :], gain, bias)
            gnorm = grad * gain
            resid = cot + inv_std * (
                gnorm
                - jnp.mean(gnorm, axis=-1, keepdims=True)
                - normed * jnp.mean(gnorm * normed, axis=-1, keepdims=True)
            )
            dr_ref[rows, :] = resid
            branch = resid.astype(BF16)
            do_s[rows, :] = branch
            dc_ref[rows, :] = dot(branch, wout_ref[...], 1, 1).astype(BF16)
            return (
                sums[0] + jnp.sum(grad * normed, axis=0, keepdims=True),
                sums[1] + jnp.sum(grad, axis=0, keepdims=True),
                sums[2] + jnp.sum(cot, axis=0, keepdims=True),
            )

        zero = jnp.zeros((1, x_ref.shape[1]), F32)
        sums = lax.fori_loop(0, tiles, finish, (zero, zero, zero))
        index = lax.broadcasted_iota(jnp.int32, (8, 1), 0)
        vecg_ref[...] = jnp.where(
            index == 0,
            sums[0],
            jnp.where(index == 1, sums[1], jnp.where(index == 2, sums[2], 0.0)),
        )
        dwout_ref[...] = dot(c_ref[...], do_s[...], 0, 0).astype(BF16)


def middle(x, cot, ctx, w_out, w_fc, w_proj, vecs, fc_bias, group):
    rows, dim = x.shape
    hidden = w_fc.shape[1]
    steps = hidden // CHUNK
    share = dim // group

    def fixed(shape):
        return pl.BlockSpec(shape, lambda c: (0,) * len(shape), pipeline_mode=pl.Buffered(1))

    return pl.pallas_call(
        middle_kernel,
        grid=(steps,),
        in_specs=[
            fixed((rows, dim)),
            fixed((rows, dim)),
            fixed((rows, dim)),
            fixed((dim, dim)),
            pl.BlockSpec((dim, CHUNK), lambda c: (0, c)),
            pl.BlockSpec((CHUNK, dim), lambda c: (c, 0)),
            fixed((8, dim)),
            pl.BlockSpec((1, 1, CHUNK), lambda c: (c, 0, 0)),
        ],
        out_specs=[
            fixed((rows, dim)),
            fixed((rows, dim)),
            fixed((rows, dim)),
            fixed((dim, dim)),
            pl.BlockSpec((group, 1, share, CHUNK), lambda c: (0, c, 0, 0)),
            pl.BlockSpec((CHUNK, dim), lambda c: (c, 0)),
            pl.BlockSpec((1, 1, CHUNK), lambda c: (c, 0, 0)),
            fixed((8, dim)),
        ],
        out_shape=[
            jax.ShapeDtypeStruct((rows, dim), BF16),
            jax.ShapeDtypeStruct((rows, dim), F32),
            jax.ShapeDtypeStruct((rows, dim), BF16),
            jax.ShapeDtypeStruct((dim, dim), BF16),
            jax.ShapeDtypeStruct((group, steps, share, CHUNK), BF16),
            jax.ShapeDtypeStruct((hidden, dim), BF16),
            jax.ShapeDtypeStruct((steps, 1, CHUNK), F32),
            jax.ShapeDtypeStruct((8, dim), F32),
        ],
        scratch_shapes=[
            pltpu.VMEM((rows, dim), F32),
            pltpu.VMEM((rows, dim), BF16),
            pltpu.VMEM((rows, dim), F32),
            pltpu.VMEM((rows, dim), F32),
            pltpu.VMEM((rows, CHUNK), BF16),
            pltpu.VMEM((rows, CHUNK), BF16),
            pltpu.VMEM((rows, dim), BF16),
        ],
        compiler_params=params(),
        cost_estimate=pl.CostEstimate(
            flops=24 * rows * dim * hidden, bytes_accessed=40_000_000, transcendentals=0
        ),
        name="middle",
    )(x, cot, ctx, w_out, w_fc, w_proj, vecs, fc_bias)


def attend(q, kv, dcol, drow, stats, ext):
    micro, tok, dim = q.shape
    total = kv.shape[1]
    pairs = dim // 128
    blocks = tok // BLK
    return pl.pallas_call(
        partial(forward_kernel, ext=ext),
        grid=(micro, pairs),
        in_specs=[
            pl.BlockSpec((1, tok, 128), lambda m, p: (m, 0, p)),
            pl.BlockSpec((1, total, 128), lambda m, p: (m, 0, p)),
            pl.BlockSpec((1, total, 128), lambda m, p: (m, 0, pairs + p)),
            pl.BlockSpec((1, ext, 1), lambda m, p: (m, 0, 0)),
            pl.BlockSpec((1, 1, ext), lambda m, p: (m, 0, 0)),
            pl.BlockSpec((1, tok, 128), lambda m, p: (m, 0, 0)),
        ],
        out_specs=[
            pl.BlockSpec((1, tok, 128), lambda m, p: (m, 0, p)),
            pl.BlockSpec((1, 2, blocks, BLK, 2 * BLK), lambda m, p: (m, p, 0, 0, 0)),
            pl.BlockSpec((1, 2, tok, total - ext), lambda m, p: (m, p, 0, 0)),
        ],
        out_shape=[
            jax.ShapeDtypeStruct((micro, tok, dim), BF16),
            jax.ShapeDtypeStruct((micro, 2 * pairs, blocks, BLK, 2 * BLK), BF16),
            jax.ShapeDtypeStruct((micro, 2 * pairs, tok, total - ext), BF16),
        ],
        compiler_params=params(),
        cost_estimate=pl.CostEstimate(
            flops=48 * micro * tok * 768 * dim, bytes_accessed=30_000_000, transcendentals=0
        ),
        name="attend",
    )(q, kv, kv, dcol, drow, stats)


def attend_back(dctx, q, kv, probs, density, stats, km, ks, mean_wide, spread_wide, ext):
    micro, tok, dim = q.shape
    total = kv.shape[1]
    pairs = dim // 128
    blocks = tok // BLK
    basis = total - ext
    part = pl.BlockSpec((1, tok, 128), lambda m, p: (m, 0, p))
    rows = pl.BlockSpec((1, total, 128), lambda m, p: (m, 0, p))
    line = pl.BlockSpec((1, 1, 128), lambda m, p: (m, 0, p))
    wide = pl.BlockSpec((basis, 128), lambda m, p: (0, p))
    return pl.pallas_call(
        partial(backward_kernel, ext=ext),
        grid=(micro, pairs),
        in_specs=[
            part,
            part,
            rows,
            pl.BlockSpec((1, total, 128), lambda m, p: (m, 0, pairs + p)),
            pl.BlockSpec((1, 2, blocks, BLK, 2 * BLK), lambda m, p: (m, p, 0, 0, 0)),
            pl.BlockSpec((1, 2, tok, basis), lambda m, p: (m, p, 0, 0)),
            pl.BlockSpec((1, tok, 128), lambda m, p: (m, 0, 0)),
            line,
            line,
            wide,
            wide,
        ],
        out_specs=[part, rows, rows, pl.BlockSpec((1, 8, 128), lambda m, p: (m, 0, p))],
        out_shape=[
            jax.ShapeDtypeStruct((micro, tok, dim), BF16),
            jax.ShapeDtypeStruct((micro, total, dim), BF16),
            jax.ShapeDtypeStruct((micro, total, dim), BF16),
            jax.ShapeDtypeStruct((micro, 8, dim), F32),
        ],
        scratch_shapes=[pltpu.VMEM((total, 128), F32), pltpu.VMEM((total, 128), F32)],
        compiler_params=params(),
        cost_estimate=pl.CostEstimate(
            flops=64 * micro * tok * 768 * dim, bytes_accessed=30_000_000, transcendentals=0
        ),
        name="attend_back",
    )(dctx, q, kv, kv, probs, density, stats, km, ks, mean_wide, spread_wide)


def on_device(
    tokens,
    cotangent,
    doc_ids,
    positions,
    w_qkv,
    w_out,
    w_fc,
    w_proj,
    ln1_gain,
    ln1_bias,
    ln2_gain,
    ln2_bias,
    fc_bias,
    proj_bias,
    mean_weight,
    spread_weight,
):
    group = lax.axis_size("fsdp")
    member = lax.axis_index("fsdp")
    micro, tok, dim = tokens.shape[0], tokens.shape[2], tokens.shape[3]
    hidden = w_fc.shape[1]
    heads = mean_weight.shape[1]
    basis = mean_weight.shape[0] * group
    head_dim = dim // heads
    seq_len = tok * group
    own_count = positions.shape[2] // group
    first_row = member * tok
    ext = tok + BLK
    x = tokens[:, 0]
    cot = cotangent[:, 0]

    onward = [(i, i + 1) for i in range(group - 1)]
    edge = lax.ppermute(x[:, tok - BLK :], "fsdp", onward)
    sample_pos = positions[:, 0]
    own_rows = lax.dynamic_slice_in_dim(sample_pos, member * own_count, own_count, 1) - first_row
    hot = (own_rows[:, :, None] == jnp.arange(tok)[None, None, :]).astype(BF16)
    picked = jnp.einsum("mst,mtd->msd", hot, x, preferred_element_type=F32).astype(BF16)
    picked = gathered(picked, "fsdp", 1)

    small = [ln1_gain, ln1_bias, ln2_gain, ln2_bias, fc_bias, proj_bias]
    small = small + [mean_weight.reshape(-1), spread_weight.reshape(-1)]
    packed = gathered(jnp.concatenate(small)[None], "fsdp", 0)
    vectors, at = [], 0
    for piece in small:
        vectors.append(packed[:, at : at + piece.shape[0]].reshape(-1).astype(F32))
        at = at + piece.shape[0]
    gain_one, bias_one, gain_two, bias_two, hidden_bias, output_bias = vectors[:6]
    mean_f32 = vectors[6].reshape(basis, heads)
    spread_f32 = vectors[7].reshape(basis, heads)
    full_qkv, full_out, full_fc, full_proj = (
        gathered_weight(w) for w in (w_qkv, w_out, w_fc, w_proj)
    )

    table = basis_rows(sample_pos, seq_len, basis)
    if sample_pos.shape[1] < basis:
        system = jnp.einsum("msn,mtn->mst", table, table, precision=HIGHEST)
        system = system + RIDGE_TERM * jnp.eye(sample_pos.shape[1], dtype=F32)
        solver = jnp.einsum("msn,mst->mnt", table, spd_inverse(system), precision=HIGHEST)
    else:
        system = jnp.einsum("msn,msk->mnk", table, table, precision=HIGHEST)
        system = system + RIDGE_TERM * jnp.eye(basis, dtype=F32)
        solver = jnp.einsum("mkn,msn->mks", spd_inverse(system), table, precision=HIGHEST)

    inputs = x.astype(F32)
    own_low = layer_norm(inputs, gain_one, bias_one)[0].astype(BF16)
    edge_low = layer_norm(edge.astype(F32), gain_one, bias_one)[0].astype(BF16)
    picked_low = layer_norm(picked.astype(F32), gain_one, bias_one)[0].astype(BF16)
    coeff = jnp.einsum("mns,msd->mnd", solver, picked_low.astype(F32), precision=HIGHEST)
    rows_low = jnp.concatenate([edge_low, own_low, coeff.astype(BF16)], axis=1)
    q = jnp.einsum(
        "mtd,de->mte", own_low, full_qkv[:, :dim], preferred_element_type=F32
    ).astype(BF16)
    kv = jnp.einsum(
        "mtd,de->mte", rows_low, full_qkv[:, dim:], preferred_element_type=F32
    ).astype(BF16)

    mean_wide = jnp.repeat(mean_f32, head_dim, axis=1)
    spread_wide = jnp.repeat(spread_f32, head_dim, axis=1)
    mem_keys = kv[:, ext:, :dim].astype(F32)
    km = jnp.sum(mem_keys * mean_wide, axis=1) * head_dim ** (-0.5)
    ks = jnp.sum(mem_keys * spread_wide, axis=1) * head_dim ** (-0.5)
    owner = (jnp.arange(dim)[:, None] // head_dim == jnp.arange(heads)[None, :]).astype(F32)
    both = jnp.concatenate([km[:, :, None] * owner, ks[:, :, None] * owner], axis=2)
    logits = jnp.einsum("mtd,mdj->mtj", q.astype(F32), both, precision=HIGHEST)
    middle_at = jax.nn.sigmoid(logits[:, :, :heads])
    basis_var = (1.25 / basis) ** 2
    spread_logit = logits[:, :, heads:]
    spread_sq = basis_var + SIGMA_SCALE * jax.nn.softplus(spread_logit)
    inv_two = 0.5 / spread_sq
    spread_slope = SIGMA_SCALE * jax.nn.sigmoid(spread_logit)
    columns = [
        middle_at,
        inv_two,
        jnp.sqrt(basis_var / spread_sq),
        -2.0 * inv_two * middle_at * (1.0 - middle_at),
        2.0 * inv_two * inv_two * spread_slope,
        -inv_two * spread_slope,
    ]
    stats = jnp.concatenate(
        [jnp.pad(c, ((0, 0), (0, 0), (0, 16 - heads))) for c in columns]
        + [jnp.zeros((micro, tok, 32), F32)],
        axis=2,
    )

    padded = jnp.concatenate([jnp.full((micro, BLK), -1, jnp.int32), doc_ids[:, 0]], axis=1)
    ext_docs = lax.dynamic_slice_in_dim(padded, first_row, ext, 1)
    ctx, probs, density = attend(
        q, kv, ext_docs[:, :, None], ext_docs[:, None, :], stats, ext
    )

    vecs = jnp.concatenate(
        [v[None] for v in (gain_two, bias_two, output_bias)] + [jnp.zeros((5, dim), F32)]
    )
    rows = micro * tok
    output, d_resid, d_ctx, dw_out, dw_fc, dw_proj, d_hidden, d_vecs = middle(
        x.reshape(rows, dim),
        cot.reshape(rows, dim),
        ctx.reshape(rows, dim),
        full_out,
        full_fc,
        full_proj,
        vecs,
        hidden_bias.reshape(-1, 1, CHUNK),
        group,
    )

    sum_proj = reduced(dw_proj.reshape(group, -1, dim), 0)
    sum_fc = reduced(dw_fc.reshape(group, -1, CHUNK), 1)

    d_q, d_k, d_v, d_sums = attend_back(
        d_ctx.reshape(micro, tok, dim),
        q,
        kv,
        probs,
        density,
        stats,
        km[:, None],
        ks[:, None],
        mean_wide,
        spread_wide,
        ext,
    )
    mean_term = jnp.sum(mem_keys * d_sums[:, 0:1], axis=0) * head_dim ** (-0.5)
    spread_term = jnp.sum(mem_keys * d_sums[:, 1:2], axis=0) * head_dim ** (-0.5)
    acc_mean = jnp.dot(mean_term, owner, precision=HIGHEST)
    acc_spread = jnp.dot(spread_term, owner, precision=HIGHEST)

    def back(grad, low, high):
        return jnp.einsum(
            "mte,de->mtd", grad, full_qkv[:, low:high], preferred_element_type=F32
        )

    d_rows = back(d_k, dim, 2 * dim) + back(d_v, 2 * dim, 3 * dim)
    returned = lax.ppermute(
        d_rows[:, :BLK].astype(BF16), "fsdp", [(i + 1, i) for i in range(group - 1)]
    )
    d_picked = jnp.einsum("mns,mnd->msd", solver, d_rows[:, ext:], precision=HIGHEST)
    d_picked = scattered(d_picked.astype(BF16), "fsdp", 1)

    def flat(value):
        return value.reshape(-1, value.shape[-1])

    dw_q = dot(flat(own_low), flat(d_q), 0, 0).astype(BF16)
    dw_k = dot(flat(rows_low), flat(d_k), 0, 0).astype(BF16)
    dw_v = dot(flat(rows_low), flat(d_v), 0, 0).astype(BF16)
    last = jnp.stack([v.reshape(group, -1, dim) for v in (dw_out, dw_q, dw_k, dw_v)], axis=1)
    sum_last = reduced(last.reshape(group, -1, dim), 0).reshape(4, -1, dim)

    d_first = d_rows[:, BLK:ext] + back(d_q, 0, dim)
    d_first = d_first + jnp.einsum("mst,msd->mtd", hot, d_picked, preferred_element_type=F32)
    d_first = d_first + jnp.pad(returned.astype(F32), ((0, 0), (tok - BLK, 0), (0, 0)))
    _, normed, inv_std = layer_norm(inputs, gain_one, bias_one)
    g_norm = d_first * gain_one
    grad_tokens = d_resid.reshape(micro, tok, dim) + inv_std * (
        g_norm
        - jnp.mean(g_norm, axis=-1, keepdims=True)
        - normed * jnp.mean(g_norm * normed, axis=-1, keepdims=True)
    )
    acc_gain_one = jnp.sum(d_first * normed, axis=(0, 1))
    acc_bias_one = jnp.sum(d_first, axis=(0, 1))

    vector_parts = [
        acc_gain_one,
        acc_bias_one,
        d_vecs[0],
        d_vecs[1],
        d_hidden,
        d_vecs[2],
        acc_mean,
        acc_spread,
    ]
    joined = jnp.concatenate([v.reshape(group, -1) for v in vector_parts], axis=1)
    own = scattered(joined, "fsdp", 0)[0]
    for bit in bits_of("rep"):
        own = own + swapped(own, "rep", bit)
    pieces, at = [], 0
    for part in vector_parts:
        size = part.size // group
        pieces.append(own[at : at + size])
        at = at + size
    share = dim // group
    grad_fc = sum_fc.reshape(hidden // CHUNK, share, CHUNK).transpose(1, 0, 2)
    grad_qkv = jnp.concatenate([sum_last[1], sum_last[2], sum_last[3]], axis=1)
    return (
        output.reshape(micro, 1, tok, dim),
        grad_tokens[:, None],
        grad_qkv.astype(F32),
        sum_last[0].astype(F32),
        grad_fc.reshape(share, hidden).astype(F32),
        sum_proj.astype(F32),
        pieces[0],
        pieces[1],
        pieces[2],
        pieces[3],
        pieces[4],
        pieces[5],
        pieces[6].reshape(-1, heads),
        pieces[7].reshape(-1, heads),
    )


def solution(mesh):
    seq = P(None, "rep", "fsdp", None)
    row = P("fsdp", None)
    vec = P("fsdp")
    return jax.shard_map(
        on_device,
        mesh=mesh,
        in_specs=(seq, seq, P(None, "rep", None), P(None, "rep", None))
        + (row, row, row, row)
        + (vec,) * 6
        + (row, row),
        out_specs=(seq, seq, row, row, row, row) + (vec,) * 6 + (row, row),
        check_vma=False,
    )
```
